256 devices in a mesh: aux: 64 (over y, z, core), blk: 4 (over x).
Axes of the slice: x: 4, y: 4, z: 8, core: 2. Of those that a mesh axis runs over, the one named last changes fastest.
Arguments:
- half_blocks: bfloat16 [32768, 64, 512], P(('aux', 'blk')), may hold values from -0.0625 to 0.0625
- screen: int32 [2048, 64], P(('aux', 'blk')), may hold values from 0 to 1, as said below
- domain_length: int32 [64], P('aux'), may hold values from 128 to 512, as said below
- domain_index: int32 [64, 512], P('aux'), may hold values from 0 to 19999, as said below
- orbital_coeff: bfloat16 [20000, 64], replicated, may hold values from -6 to 6
Outputs:
- exchange_block: float32 [64, 512, 512], P('aux', 'blk')
- exchange_orbital: float32 [64, 64, 512], P('aux', None, 'blk')
The draws below stay inside these ranges and needn't reach their ends.
Inputs may be any that keep to these rules, and one draw needn't show every extreme that they name: `screen`: within every aligned run of 8 tiles each orbital keeps at least 2 and at most 4 tiles; one orbital keeps exactly 4 in every run. `domain_length`: some orbital's domain is full. `domain_index`: each orbital's row holds distinct basis functions in increasing order.
All inputs are finite; a program needn't handle non-finite values.
Results may differ from the reference program's by a relative error of at most 0.00045.
Values may be sent and summed in bfloat16 or wider, within the bound.
No kernel may reach another device: no remote copies, remote signals or barrier semaphores. Data moves between devices by JAX's collectives and lax.ppermute only.
A program may use at most 64 MiB of HBM per device.

```python
import jax
import jax.numpy as jnp
from jax import lax

DOM = 512
NBAS = 20000
TILE = 16
ST = 8
KEEP = 4
ORB = 64
NAUX = 32768
NTILE = 2048


def draw_screen(key, part):
    slab_count = NTILE // ST
    key_count, key_full, key_score = jax.random.split(jax.random.fold_in(key, 11), 3)
    least = max(1, KEEP // 2)
    counts = jax.random.randint(key_count, (slab_count, ORB), least, KEEP + 1)
    full_orbital = jax.random.randint(key_full, (), 0, ORB)
    counts = jnp.where(jnp.arange(ORB)[None, :] == full_orbital, KEEP, counts)
    scores = jax.random.randint(key_score, (slab_count, ST, ORB), 0, 1 << 20) * ST + jnp.arange(ST, dtype=jnp.int32)[None, :, None]
    tile_rank = jnp.argsort(jnp.argsort(scores, axis=1), axis=1)
    kept_tiles = (tile_rank < counts[:, None, :]).astype(jnp.int32)
    return kept_tiles.reshape(NTILE, ORB)


def draw_domain_length(key, part):
    key_len, key_full = jax.random.split(jax.random.fold_in(key, 23), 2)
    lengths = jax.random.randint(key_len, (ORB,), DOM // 4, DOM + 1)
    full_orbital = jax.random.randint(key_full, (), 0, ORB)
    return jnp.where(jnp.arange(ORB) == full_orbital, DOM, lengths).astype(jnp.int32)


def draw_domain_index(key, part):
    key_start, key_step = jax.random.split(jax.random.fold_in(key, 37), 2)
    starts = jax.random.randint(key_start, (ORB,), 0, NBAS - 2 * DOM + 1)
    steps_bits = jax.random.randint(key_step, (ORB, DOM), 0, 2)
    return (starts[:, None] + 2 * jnp.arange(DOM, dtype=jnp.int32)[None, :] + steps_bits).astype(jnp.int32)


def level_of(stream_key, dims, pieces, low, largest):
    def one(dim, parts):
        draws = jax.random.uniform(jax.random.fold_in(jax.random.fold_in(stream_key, 6), dim), (parts,), jnp.float32, low / len(pieces), largest / len(pieces))
        return jnp.repeat(jnp.exp(draws), dims[dim] // parts).reshape((-1,) + (1,) * (len(dims) - dim - 1))

    level = one(*pieces[0])
    for cut in pieces[1:]:
        level = level * one(*cut)
    return level


def bell_draw(rng, shape, deviation, most, pieces=(), held_as=jnp.bfloat16):
    entries = deviation * jax.random.normal(rng, shape, jnp.float32)
    if pieces:
        entries = entries * level_of(rng, shape, pieces, -0.22, 0.18)
    return jnp.clip(entries, -most, most).astype(held_as)


def setup_inputs(seed: int = 0) -> dict:
    streams_of = jax.random.split(jax.random.key(seed), 6)
    half_blocks = bell_draw(streams_of[0], (NAUX, ORB, DOM), (NAUX // 4) ** -0.5, 0.0625, ((0, 256),))
    screen = draw_screen(jax.random.fold_in(streams_of[5], 71), 0)
    domain_length = draw_domain_length(jax.random.fold_in(streams_of[5], 71), 0)
    domain_index = draw_domain_index(jax.random.fold_in(streams_of[5], 71), 0)
    orbital_coeff = bell_draw(streams_of[4], (NBAS, ORB), 1.0, 6.0)
    return {"half_blocks": half_blocks, "screen": screen, "domain_length": domain_length, "domain_index": domain_index, "orbital_coeff": orbital_coeff}


def reference(half_blocks, screen, domain_length, domain_index, orbital_coeff):
    def per_orbital(orbital):
        columns = lax.dynamic_index_in_dim(half_blocks, orbital, 1, keepdims=False)
        row_keep = jnp.repeat(lax.dynamic_index_in_dim(screen, orbital, 1, keepdims=False), TILE)
        masked = columns * row_keep.astype(jnp.bfloat16)[:, None]
        gram_full = jnp.dot(masked.T, masked, preferred_element_type=jnp.float32)
        length = domain_length[orbital]
        inside = (jnp.arange(DOM, dtype=jnp.int32) < length).astype(jnp.float32)
        exch_block = gram_full * inside[:, None] * inside[None, :]
        local_coeff = jnp.take(orbital_coeff, domain_index[orbital], axis=0).astype(jnp.float32)
        occ_block = jnp.dot(local_coeff.T, exch_block, precision=lax.Precision.HIGHEST)
        return exch_block, occ_block

    exchange_block, exchange_orbital = lax.map(per_orbital, jnp.arange(ORB, dtype=jnp.int32))
    return exchange_block, exchange_orbital
```

```python
import jax
import jax.numpy as jnp
from jax import lax
from jax.experimental import pallas as pl
from jax.experimental.pallas import tpu as pltpu
from jax.sharding import Mesh
from jax.sharding import PartitionSpec as P

TILES = 8
SLOTS = 4
TROWS = 16
HALF = 8
OG = 8
SHARES = 4
NONE = -1000


def pack_kernel(code_ref, x_ref, o_ref, pick_ref):
    step = pl.program_id(0)
    width = TILES * HALF * OG
    place = lax.broadcasted_iota(jnp.int32, (HALF, width), 1) - OG * lax.broadcasted_iota(
        jnp.int32, (HALF, width), 0
    )
    for i in range(OG):
        for k in range(0, SLOTS, 2):
            pair = [
                jnp.where(place == code_ref[k + d, step * OG + i], 1.0, 0.0) for d in range(2)
            ]
            row = (i * SLOTS + k) * HALF
            pick_ref[row : row + 2 * HALF, :] = jnp.concatenate(pair, axis=0).astype(jnp.bfloat16)
    for h in range(2):
        rows = x_ref[:, h].astype(jnp.float32).reshape(width, x_ref.shape[-1]).astype(jnp.bfloat16)
        got = jnp.dot(pick_ref[...], rows, preferred_element_type=jnp.float32)
        got = got.astype(jnp.bfloat16).reshape(OG, SLOTS * HALF, x_ref.shape[-1])
        o_ref[:, h * SLOTS * HALF : (h + 1) * SLOTS * HALF, :] = got


def pack(code, half_blocks):
    rows, orbitals, width = half_blocks.shape
    tiled = half_blocks.reshape(TILES, 2, HALF, orbitals, width)
    kept = rows // TILES * SLOTS
    return pl.pallas_call(
        pack_kernel,
        grid_spec=pltpu.PrefetchScalarGridSpec(
            num_scalar_prefetch=1,
            grid=(orbitals // OG,),
            in_specs=[pl.BlockSpec((TILES, 2, HALF, OG, width), lambda s, c: (0, 0, 0, s, 0))],
            out_specs=pl.BlockSpec((OG, kept, width), lambda s, c: (s, 0, 0)),
            scratch_shapes=[pltpu.VMEM((OG * SLOTS * HALF, TILES * HALF * OG), jnp.bfloat16)],
        ),
        out_shape=jax.ShapeDtypeStruct((orbitals, kept, width), jnp.bfloat16),
    )(code, tiled)


def gram_kernel(first_ref, x_ref, *refs):
    outs, acc = refs[:-1], refs[-1]
    step = pl.program_id(0)
    x = x_ref[...]
    part = lax.dot_general(x, x, (((0,), (0,)), ((), ())), preferred_element_type=jnp.float32)

    @pl.when(step == 0)
    def _():
        acc[...] = part

    @pl.when(step > 0)
    def _():
        acc[...] += part

    @pl.when(step == pl.num_programs(0) - 1)
    def _():
        share = acc.shape[0] // SHARES
        for j in range(SHARES):
            start = pl.multiple_of(((first_ref[0] + j) % SHARES) * share, share)
            outs[j][...] = acc[pl.ds(start, share), :]


def gram(first, columns, depth=1024):
    rows, width = columns.shape
    share = width // SHARES
    return pl.pallas_call(
        gram_kernel,
        grid_spec=pltpu.PrefetchScalarGridSpec(
            num_scalar_prefetch=1,
            grid=(rows // depth,),
            in_specs=[pl.BlockSpec((depth, width), lambda s, f: (s, 0))],
            out_specs=[pl.BlockSpec((share, width), lambda s, f: (0, 0))] * SHARES,
            scratch_shapes=[pltpu.VMEM((width, width), jnp.float32)],
        ),
        out_shape=[jax.ShapeDtypeStruct((share, width), jnp.float32)] * SHARES,
    )(first, columns)


def slot_codes(screen):
    seen = jnp.zeros_like(screen[0])
    codes = [jnp.full_like(screen[0], NONE) for _ in range(SLOTS)]
    inner = lax.iota(jnp.int32, screen.shape[1]) % OG
    for t in range(TILES):
        kept = screen[t] == 1
        for k in range(SLOTS):
            codes[k] = jnp.where(kept & (seen == k), t * HALF * OG + inner, codes[k])
        seen = seen + screen[t]
    return jnp.stack(codes)


def per_device(half_blocks, screen, domain_length, domain_index, orbital_coeff):
    dom_width = half_blocks.shape[2]
    packed = pack(slot_codes(screen), half_blocks)
    arrived = lax.all_to_all(packed, ("y", "x", "zl", "c"), split_axis=0, concat_axis=0, tiled=True)
    columns = arrived.reshape(-1, dom_width)
    shares = gram(lax.axis_index("zh").reshape(1), columns)
    total = None
    for j, share in enumerate(shares):
        route = [(g * 4 + x, x * 4 + (g + j) % 4) for g in range(4) for x in range(4)]
        got = lax.ppermute(share, ("zh", "x"), route)
        total = got if total is None else total + got
    row_share = dom_width // SHARES
    length = domain_length[0]
    row_place = lax.axis_index("x") * row_share + lax.iota(jnp.int32, row_share)
    col_place = lax.iota(jnp.int32, dom_width)
    inside = ((row_place < length)[:, None] & (col_place < length)[None, :]).astype(jnp.float32)
    exch_rows = total * inside
    local_coeff = jnp.take(orbital_coeff, domain_index[0], axis=0).astype(jnp.float32)
    occ_rows = jnp.einsum("ab,bj->ja", exch_rows, local_coeff, precision=lax.Precision.HIGHEST)
    return (exch_rows[None], occ_rows[None])


def solution(mesh):
    split = Mesh(mesh.devices.reshape(4, 4, 2, 2, 4), ("y", "zh", "zl", "c", "x"))
    aux = ("y", "zh", "zl", "c")
    every = aux + ("x",)
    return jax.shard_map(
        per_device,
        mesh=split,
        in_specs=(P(every, None, None), P(every, None), P(aux), P(aux, None), P()),
        out_specs=(P(aux, "x", None), P(aux, None, "x")),
        check_vma=False,
    )
```

```python
import jax
import jax.numpy as jnp
from jax import lax
from jax.experimental import pallas as pl
from jax.experimental.pallas import tpu as pltpu
from jax.sharding import Mesh
from jax.sharding import PartitionSpec as P

TILES = 8
SLOTS = 4
PART = 4
PARTS = 4
OG = 16
SHARES = 4
NONE = -1000


def code_kernel(screen_ref, o_ref):
    seen = jnp.zeros_like(screen_ref[0:1, :])
    inner = lax.broadcasted_iota(jnp.int32, seen.shape, 1) % OG
    codes = [jnp.full_like(seen, NONE) for _ in range(SLOTS)]
    for t in range(TILES):
        kept = screen_ref[t : t + 1, :]
        for k in range(SLOTS):
            here = (kept == 1) & (seen == k)
            codes[k] = jnp.where(here, t * PART * OG + inner, codes[k])
        seen = seen + kept
    for k in range(SLOTS):
        o_ref[k : k + 1, :] = codes[k]


def slot_codes(screen):
    return pl.pallas_call(
        code_kernel, out_shape=jax.ShapeDtypeStruct((SLOTS, screen.shape[1]), jnp.int32)
    )(screen)


def pack_kernel(code_ref, group_ref, x_ref, o_ref, pick_ref):
    step = pl.program_id(0)
    width = TILES * PART * OG
    row = lax.broadcasted_iota(jnp.int32, (2 * PART, width), 0)
    place = lax.broadcasted_iota(jnp.int32, (2 * PART, width), 1) - OG * (row % PART)
    for i in range(OG):
        both = []
        for k in range(0, SLOTS, 2):
            first, second = (code_ref[k + d, step * OG + i] for d in range(2))
            both.append(jnp.where(place == jnp.where(row < PART, first, second), 1.0, 0.0))
        at = i * SLOTS * PART
        pick_ref[at : at + SLOTS * PART, :] = jnp.concatenate(both, axis=0).astype(jnp.bfloat16)
    for h in range(PARTS):
        rows = x_ref[:, h].reshape(width, x_ref.shape[-1])
        got = jnp.dot(pick_ref[...], rows, preferred_element_type=jnp.float32).astype(jnp.bfloat16)
        for i in range(OG):
            low = i % 4
            slot = ((i // 4 - low - group_ref[0] + 8) % 4) * 4 + low
            at = i * SLOTS * PART
            o_ref[slot, h * SLOTS * PART : (h + 1) * SLOTS * PART, :] = got[at : at + SLOTS * PART]


def pack(code, group, half_blocks):
    rows, orbitals, width = half_blocks.shape
    tiled = half_blocks.reshape(TILES, PARTS, PART, orbitals, width)
    kept = rows // TILES * SLOTS
    return pl.pallas_call(
        pack_kernel,
        grid_spec=pltpu.PrefetchScalarGridSpec(
            num_scalar_prefetch=2,
            grid=(orbitals // OG,),
            in_specs=[
                pl.BlockSpec((TILES, PARTS, PART, OG, width), lambda s, c, g: (0, 0, 0, s, 0))
            ],
            out_specs=pl.BlockSpec((OG, kept, width), lambda s, c, g: (s, 0, 0)),
            scratch_shapes=[pltpu.VMEM((OG * SLOTS * PART, TILES * PART * OG), jnp.bfloat16)],
        ),
        out_shape=jax.ShapeDtypeStruct((orbitals, kept, width), jnp.bfloat16),
    )(code, group, tiled)


def gram_kernel(first_ref, x_ref, *refs):
    outs, acc = refs[:-1], refs[-1]
    step = pl.program_id(0)
    x = x_ref[...]
    part = lax.dot_general(x, x, (((0,), (0,)), ((), ())), preferred_element_type=jnp.float32)

    @pl.when(step == 0)
    def _():
        acc[...] = part

    @pl.when(step > 0)
    def _():
        acc[...] += part

    @pl.when(step == pl.num_programs(0) - 1)
    def _():
        share = acc.shape[0] // SHARES
        for j in range(SHARES):
            start = pl.multiple_of(((first_ref[0] + j) % SHARES) * share, share)
            outs[j][...] = acc[pl.ds(start, share), :]


def gram(first, columns, depth=1024):
    rows, width = columns.shape
    share = width // SHARES
    return pl.pallas_call(
        gram_kernel,
        grid_spec=pltpu.PrefetchScalarGridSpec(
            num_scalar_prefetch=1,
            grid=(rows // depth,),
            in_specs=[pl.BlockSpec((depth, width), lambda s, f: (s, 0))],
            out_specs=[pl.BlockSpec((share, width), lambda s, f: (0, 0))] * SHARES,
            scratch_shapes=[pltpu.VMEM((width, width), jnp.float32)],
        ),
        out_shape=[jax.ShapeDtypeStruct((share, width), jnp.float32)] * SHARES,
    )(first, columns)


def routes(j):
    pairs = []
    for g in range(4):
        for low in range(4):
            for x in range(4):
                owner = (x + g + low) % 4
                pairs.append(((g * 4 + low) * 4 + x, (owner * 4 + low) * 4 + (x + j) % 4))
    return pairs


def per_device(half_blocks, screen, domain_length, domain_index, orbital_coeff):
    dom_width = half_blocks.shape[2]
    group = lax.axis_index("zh").reshape(1)
    packed = pack(slot_codes(screen), group, half_blocks)
    arrived = lax.all_to_all(packed, ("y", "x", "zl", "c"), split_axis=0, concat_axis=0, tiled=True)
    columns = arrived.reshape(-1, dom_width)
    shares = gram(lax.axis_index("x").reshape(1), columns)
    total = None
    for j, share in enumerate(shares):
        got = lax.ppermute(share, ("zh", "zl", "c", "x"), routes(j))
        total = got if total is None else total + got
    row_share = dom_width // SHARES
    length = domain_length[0]
    row_place = lax.axis_index("x") * row_share + lax.iota(jnp.int32, row_share)
    col_place = lax.iota(jnp.int32, dom_width)
    inside = ((row_place < length)[:, None] & (col_place < length)[None, :]).astype(jnp.float32)
    exch_rows = total * inside
    local_coeff = jnp.take(orbital_coeff, domain_index[0], axis=0).astype(jnp.float32)
    occ_rows = jnp.einsum("ab,bj->ja", exch_rows, local_coeff, precision=lax.Precision.HIGHEST)
    return (exch_rows[None], occ_rows[None])


def solution(mesh):
    split = Mesh(mesh.devices.reshape(4, 4, 2, 2, 4), ("y", "zh", "zl", "c", "x"))
    aux = ("y", "zh", "zl", "c")
    every = aux + ("x",)
    return jax.shard_map(
        per_device,
        mesh=split,
        in_specs=(P(every, None, None), P(every, None), P(aux), P(aux, None), P()),
        out_specs=(P(aux, "x", None), P(aux, None, "x")),
        check_vma=False,
    )
```

```python
import jax
import jax.numpy as jnp
from jax import lax
from jax.experimental import pallas as pl
from jax.experimental.pallas import tpu as pltpu
from jax.sharding import Mesh
from jax.sharding import PartitionSpec as P

TILES = 8
SLOTS = 4
PART = 4
PARTS = 4
OG = 16
SHARES = 4
NONE = -1000


def code_kernel(screen_ref, o_ref):
    seen = jnp.zeros_like(screen_ref[0:1, :])
    inner = lax.broadcasted_iota(jnp.int32, seen.shape, 1) % OG
    codes = [jnp.full_like(seen, NONE) for _ in range(SLOTS)]
    for t in range(TILES):
        kept = screen_ref[t : t + 1, :]
        for k in range(SLOTS):
            here = (kept == 1) & (seen == k)
            codes[k] = jnp.where(here, t * PART * OG + inner, codes[k])
        seen = seen + kept
    for k in range(SLOTS):
        o_ref[k : k + 1, :] = codes[k]


def slot_codes(screen):
    return pl.pallas_call(
        code_kernel, out_shape=jax.ShapeDtypeStruct((SLOTS, screen.shape[1]), jnp.int32)
    )(screen)


def holder(zh, low, g):
    away = (zh - g) & 3
    return (away + 2 * (g & 1) * (1 - (away & 1)) - low) & 3


def pack_kernel(code_ref, group_ref, x_hbm, o_hbm, x_ref, o_ref, pick_ref, in_sems, out_sems):
    steps = x_hbm.shape[3] // OG
    arrivals = [
        pltpu.make_async_copy(
            x_hbm.at[:, :, :, s * OG : (s + 1) * OG, :], x_ref.at[s], in_sems.at[s]
        )
        for s in range(steps)
    ]
    leaving = [
        pltpu.make_async_copy(
            o_ref.at[s * OG : (s + 1) * OG], o_hbm.at[s * OG : (s + 1) * OG], out_sems.at[s]
        )
        for s in range(steps)
    ]
    for copy in arrivals:
        copy.start()
    slots = [holder(i // 4, i % 4, group_ref[0]) * 4 + i % 4 for i in range(OG)]
    width = TILES * PART * OG
    row = lax.broadcasted_iota(jnp.int32, (2 * PART, width), 0)
    place = lax.broadcasted_iota(jnp.int32, (2 * PART, width), 1) - OG * (row % PART)
    for s in range(steps):
        for i in range(OG):
            both = []
            for k in range(0, SLOTS, 2):
                first, second = (code_ref[k + d, s * OG + i] for d in range(2))
                both.append(jnp.where(place == jnp.where(row < PART, first, second), 1.0, 0.0))
            at = i * SLOTS * PART
            pick_ref[at : at + SLOTS * PART, :] = jnp.concatenate(both, axis=0).astype(jnp.bfloat16)
        arrivals[s].wait()
        for h in range(PARTS):
            rows = x_ref[s, :, h].reshape(width, x_ref.shape[-1])
            got = jnp.dot(pick_ref[...], rows, preferred_element_type=jnp.float32)
            got = got.astype(jnp.bfloat16)
            for i in range(OG):
                at = i * SLOTS * PART
                to = h * SLOTS * PART
                o_ref[s * OG + slots[i], to : to + SLOTS * PART, :] = got[at : at + SLOTS * PART]
        leaving[s].start()
    for copy in leaving:
        copy.wait()


def pack(code, group, half_blocks):
    rows, orbitals, width = half_blocks.shape
    tiled = half_blocks.reshape(TILES, PARTS, PART, orbitals, width)
    kept = rows // TILES * SLOTS
    steps = orbitals // OG
    return pl.pallas_call(
        pack_kernel,
        in_specs=[
            pl.BlockSpec(memory_space=pltpu.SMEM),
            pl.BlockSpec(memory_space=pltpu.SMEM),
            pl.BlockSpec(memory_space=pl.ANY),
        ],
        out_specs=pl.BlockSpec(memory_space=pl.ANY),
        out_shape=jax.ShapeDtypeStruct((orbitals, kept, width), jnp.bfloat16),
        scratch_shapes=[
            pltpu.VMEM((steps, TILES, PARTS, PART, OG, width), jnp.bfloat16),
            pltpu.VMEM((orbitals, kept, width), jnp.bfloat16),
            pltpu.VMEM((OG * SLOTS * PART, TILES * PART * OG), jnp.bfloat16),
            pltpu.SemaphoreType.DMA((steps,)),
            pltpu.SemaphoreType.DMA((steps,)),
        ],
    )(code, group, tiled)


def gram_kernel(first_ref, x_hbm, *refs):
    outs, x_ref, acc, sems = refs[:SHARES], refs[-3], refs[-2], refs[-1]
    parts = sems.shape[0]
    depth = x_hbm.shape[0] // parts
    arrivals = [
        pltpu.make_async_copy(
            x_hbm.at[p * depth : (p + 1) * depth], x_ref.at[p * depth : (p + 1) * depth], sems.at[p]
        )
        for p in range(parts)
    ]
    for copy in arrivals:
        copy.start()
    for p in range(parts):
        arrivals[p].wait()
        x = x_ref[p * depth : (p + 1) * depth, :]
        part = lax.dot_general(x, x, (((0,), (0,)), ((), ())), preferred_element_type=jnp.float32)
        if p == 0:
            acc[...] = part
        else:
            acc[...] += part
    share = acc.shape[0] // SHARES
    for j in range(SHARES):
        start = pl.multiple_of(((first_ref[0] + j) % SHARES) * share, share)
        outs[j][...] = acc[pl.ds(start, share), :]


def gram(first, columns, parts=4):
    rows, width = columns.shape
    share = width // SHARES
    return pl.pallas_call(
        gram_kernel,
        in_specs=[pl.BlockSpec(memory_space=pltpu.SMEM), pl.BlockSpec(memory_space=pl.ANY)],
        out_specs=[pl.BlockSpec(memory_space=pltpu.VMEM)] * SHARES,
        out_shape=[jax.ShapeDtypeStruct((share, width), jnp.float32)] * SHARES,
        scratch_shapes=[
            pltpu.VMEM((rows, width), jnp.bfloat16),
            pltpu.VMEM((width, width), jnp.float32),
            pltpu.SemaphoreType.DMA((parts,)),
        ],
    )(first, columns)


def routes(j):
    pairs = []
    for g in range(4):
        for low in range(4):
            for owner in range(4):
                x = holder(owner, low, g)
                pairs.append(((g * 4 + low) * 4 + x, (owner * 4 + low) * 4 + (x + j) % 4))
    return pairs


def per_device(half_blocks, screen, domain_length, domain_index, orbital_coeff):
    dom_width = half_blocks.shape[2]
    group = lax.axis_index("zh").reshape(1)
    packed = pack(slot_codes(screen), group, half_blocks)
    arrived = lax.all_to_all(packed, ("y", "x", "zl", "c"), split_axis=0, concat_axis=0, tiled=True)
    columns = arrived.reshape(-1, dom_width)
    shares = gram(lax.axis_index("x").reshape(1), columns)
    total = None
    for j, share in enumerate(shares):
        got = lax.ppermute(share, ("zh", "zl", "c", "x"), routes(j))
        total = got if total is None else total + got
    row_share = dom_width // SHARES
    length = domain_length[0]
    row_place = lax.axis_index("x") * row_share + lax.iota(jnp.int32, row_share)
    col_place = lax.iota(jnp.int32, dom_width)
    inside = ((row_place < length)[:, None] & (col_place < length)[None, :]).astype(jnp.float32)
    exch_rows = total * inside
    local_coeff = jnp.take(orbital_coeff, domain_index[0], axis=0).astype(jnp.float32)
    occ_rows = jnp.einsum("ab,bj->ja", exch_rows, local_coeff, precision=lax.Precision.HIGHEST)
    return (exch_rows[None], occ_rows[None])


def solution(mesh):
    split = Mesh(mesh.devices.reshape(4, 4, 2, 2, 4), ("y", "zh", "zl", "c", "x"))
    aux = ("y", "zh", "zl", "c")
    every = aux + ("x",)
    return jax.shard_map(
        per_device,
        mesh=split,
        in_specs=(P(every, None, None), P(every, None), P(aux), P(aux, None), P()),
        out_specs=(P(aux, "x", None), P(aux, None, "x")),
        check_vma=False,
    )
```

```python
import jax
import jax.numpy as jnp
from jax import lax
from jax.experimental import pallas as pl
from jax.experimental.pallas import tpu as pltpu
from jax.sharding import Mesh
from jax.sharding import PartitionSpec as P

TILES = 8
SLOTS = 4
PART = 4
PARTS = 4
OG = 16
SHARES = 4
SHIFTS = (2, 1, 3, 0)
NONE = -1000


def holder(zh, low, g):
    away = (zh - g) & 3
    return (away + 2 * (g & 1) * (1 - (away & 1)) - low) & 3


def slot_codes(screen_ref, code_ref, orbital):
    for k in range(SLOTS):
        code_ref[k, orbital] = NONE
    seen = 0
    for t in range(TILES):
        code_ref[seen, orbital] = t * PART * OG + orbital % OG
        seen = seen + screen_ref[t, orbital]
    code_ref[seen, orbital] = NONE


def pack_kernel(
    screen_ref, group_ref, x_hbm, o_hbm, x_ref, o_ref, pick_ref, code_ref, in_sems, out_sems
):
    steps = x_hbm.shape[3] // OG
    arrivals = [
        pltpu.make_async_copy(
            x_hbm.at[:, :, :, s * OG : (s + 1) * OG, :], x_ref.at[s], in_sems.at[s]
        )
        for s in range(steps)
    ]
    runs = [[(zl * steps + s) * 8 for zl in range(2)] for s in range(steps)]
    leaving = [
        pltpu.make_async_copy(
            o_ref.at[run : run + 8], o_hbm.at[run : run + 8], out_sems.at[run // 8]
        )
        for s in range(steps)
        for run in runs[s]
    ]
    for copy in arrivals:
        copy.start()
    slots = [holder(i // 4, i % 4, group_ref[0]) * 2 + i % 2 for i in range(OG)]
    width = TILES * PART * OG
    row = lax.broadcasted_iota(jnp.int32, (2 * PART, width), 0)
    place = lax.broadcasted_iota(jnp.int32, (2 * PART, width), 1) - OG * (row % PART)
    for s in range(steps):
        for i in range(OG):
            slot_codes(screen_ref, code_ref, s * OG + i)
        for i in range(OG):
            both = []
            for k in range(0, SLOTS, 2):
                first, second = (code_ref[k + d, s * OG + i] for d in range(2))
                both.append(jnp.where(place == jnp.where(row < PART, first, second), 1.0, 0.0))
            at = i * SLOTS * PART
            pick_ref[at : at + SLOTS * PART, :] = jnp.concatenate(both, axis=0).astype(jnp.bfloat16)
        arrivals[s].wait()
        for h in range(PARTS):
            rows = x_ref[s, :, h].reshape(width, x_ref.shape[-1])
            got = jnp.dot(pick_ref[...], rows, preferred_element_type=jnp.float32)
            got = got.astype(jnp.bfloat16)
            for i in range(OG):
                at = i * SLOTS * PART
                to = h * SLOTS * PART
                o_ref[runs[s][i % 4 // 2] + slots[i], to : to + SLOTS * PART, :] = got[at : at + SLOTS * PART]
        for copy in leaving[2 * s : 2 * s + 2]:
            copy.start()
    for copy in leaving:
        copy.wait()


def pack(screen, group, half_blocks):
    rows, orbitals, width = half_blocks.shape
    tiled = half_blocks.reshape(TILES, PARTS, PART, orbitals, width)
    kept = rows // TILES * SLOTS
    steps = orbitals // OG
    return pl.pallas_call(
        pack_kernel,
        in_specs=[
            pl.BlockSpec(memory_space=pltpu.SMEM),
            pl.BlockSpec(memory_space=pltpu.SMEM),
            pl.BlockSpec(memory_space=pl.ANY),
        ],
        out_specs=pl.BlockSpec(memory_space=pl.ANY),
        out_shape=jax.ShapeDtypeStruct((orbitals, kept, width), jnp.bfloat16),
        scratch_shapes=[
            pltpu.VMEM((steps, TILES, PARTS, PART, OG, width), jnp.bfloat16),
            pltpu.VMEM((orbitals, kept, width), jnp.bfloat16),
            pltpu.VMEM((OG * SLOTS * PART, TILES * PART * OG), jnp.bfloat16),
            pltpu.SMEM((TILES + 1, orbitals), jnp.int32),
            pltpu.SemaphoreType.DMA((steps,)),
            pltpu.SemaphoreType.DMA((2 * steps,)),
        ],
    )(screen, group, tiled)


def gram_kernel(first_ref, x_hbm, *refs):
    outs, x_ref, acc, sems = refs[:SHARES], refs[-3], refs[-2], refs[-1]
    parts = sems.shape[0]
    depth = x_hbm.shape[0] // parts
    arrivals = [
        pltpu.make_async_copy(
            x_hbm.at[p * depth : (p + 1) * depth], x_ref.at[p * depth : (p + 1) * depth], sems.at[p]
        )
        for p in range(parts)
    ]
    for copy in arrivals:
        copy.start()
    for p in range(parts):
        arrivals[p].wait()
        x = x_ref[p * depth : (p + 1) * depth, :]
        part = lax.dot_general(x, x, (((0,), (0,)), ((), ())), preferred_element_type=jnp.float32)
        if p == 0:
            acc[...] = part
        else:
            acc[...] += part
    share = acc.shape[0] // SHARES
    for j, shift in enumerate(SHIFTS):
        start = pl.multiple_of(((first_ref[0] + shift) % SHARES) * share, share)
        outs[j][...] = acc[pl.ds(start, share), :]


def gram(first, columns, parts=4):
    rows, width = columns.shape
    share = width // SHARES
    return pl.pallas_call(
        gram_kernel,
        in_specs=[pl.BlockSpec(memory_space=pltpu.SMEM), pl.BlockSpec(memory_space=pl.ANY)],
        out_specs=[pl.BlockSpec(memory_space=pltpu.VMEM)] * SHARES,
        out_shape=[jax.ShapeDtypeStruct((share, width), jnp.float32)] * SHARES,
        scratch_shapes=[
            pltpu.VMEM((rows, width), jnp.bfloat16),
            pltpu.VMEM((width, width), jnp.float32),
            pltpu.SemaphoreType.DMA((parts,)),
        ],
    )(first, columns)


def routes(j):
    pairs = []
    for g in range(4):
        for low in range(4):
            for owner in range(4):
                x = holder(owner, low, g)
                pairs.append(((g * 4 + low) * 4 + x, (owner * 4 + low) * 4 + (x + j) % 4))
    return pairs


def per_device(half_blocks, screen, domain_length, domain_index, orbital_coeff):
    dom_width = half_blocks.shape[2]
    group = lax.axis_index("zh").reshape(1)
    packed = pack(screen, group, half_blocks)
    arrived = lax.all_to_all(packed, ("zl", "y", "x", "c"), split_axis=0, concat_axis=0, tiled=True)
    columns = arrived.reshape(-1, dom_width)
    shares = gram(lax.axis_index("x").reshape(1), columns)
    total = None
    for share, shift in zip(shares, SHIFTS):
        got = lax.ppermute(share, ("zh", "zl", "c", "x"), routes(shift))
        total = got if total is None else total + got
    row_share = dom_width // SHARES
    length = domain_length[0]
    row_place = lax.axis_index("x") * row_share + lax.iota(jnp.int32, row_share)
    col_place = lax.iota(jnp.int32, dom_width)
    inside = ((row_place < length)[:, None] & (col_place < length)[None, :]).astype(jnp.float32)
    exch_rows = total * inside
    local_coeff = jnp.take(orbital_coeff, domain_index[0], axis=0).astype(jnp.float32)
    occ_rows = jnp.einsum("ab,bj->ja", exch_rows, local_coeff, precision=lax.Precision.HIGHEST)
    return (exch_rows[None], occ_rows[None])


def solution(mesh):
    split = Mesh(mesh.devices.reshape(4, 4, 2, 2, 4), ("y", "zh", "zl", "c", "x"))
    aux = ("y", "zh", "zl", "c")
    every = aux + ("x",)
    return jax.shard_map(
        per_device,
        mesh=split,
        in_specs=(P(every, None, None), P(every, None), P(aux), P(aux, None), P()),
        out_specs=(P(aux, "x", None), P(aux, None, "x")),
        check_vma=False,
    )
```

```python
import jax
import jax.numpy as jnp
from jax import lax
from jax.experimental import pallas as pl
from jax.experimental.pallas import tpu as pltpu
from jax.sharding import Mesh
from jax.sharding import PartitionSpec as P

TILES = 8
SLOTS = 4
PART = 4
PARTS = 4
OG = 16
SHARES = 4
SHIFTS = (2, 1, 3, 0)
NONE = -1000


def holder(zh, zl, c, g):
    away = (zh - g) & 3
    turn = (away + 1) & 3 if zl else away ^ 1
    return (1 - (away >> 1) if zl else (away ^ (away >> 1)) & 1), (turn - 2 * c) & 3


def slot_codes(screen_ref, code_ref, orbital):
    for k in range(SLOTS):
        code_ref[k, orbital] = NONE
    seen = 0
    for t in range(TILES):
        code_ref[seen, orbital] = t * PART * OG + orbital % OG
        seen = seen + screen_ref[t, orbital]
    code_ref[seen, orbital] = NONE


def pack_kernel(
    screen_ref, group_ref, x_hbm, o_hbm, x_ref, o_ref, pick_ref, code_ref, in_sems, out_sems
):
    steps = x_hbm.shape[3] // OG
    arrivals = [
        pltpu.make_async_copy(
            x_hbm.at[:, :, :, s * OG : (s + 1) * OG, :], x_ref.at[s], in_sems.at[s]
        )
        for s in range(steps)
    ]
    runs = [[(zl * steps + s) * 8 for zl in range(2)] for s in range(steps)]
    leaving = [
        pltpu.make_async_copy(
            o_ref.at[run : run + 8], o_hbm.at[run : run + 8], out_sems.at[run // 8]
        )
        for s in range(steps)
        for run in runs[s]
    ]
    for copy in arrivals:
        copy.start()
    slots = []
    for i in range(OG):
        pair, x = holder(i // 4, i // 2 % 2, i % 2, group_ref[0])
        slots.append(pair * steps * 8 + x * 2 + i % 2)
    width = TILES * PART * OG
    row = lax.broadcasted_iota(jnp.int32, (2 * PART, width), 0)
    place = lax.broadcasted_iota(jnp.int32, (2 * PART, width), 1) - OG * (row % PART)
    for s in range(steps):
        for i in range(OG):
            slot_codes(screen_ref, code_ref, s * OG + i)
        for i in range(OG):
            both = []
            for k in range(0, SLOTS, 2):
                first, second = (code_ref[k + d, s * OG + i] for d in range(2))
                both.append(jnp.where(place == jnp.where(row < PART, first, second), 1.0, 0.0))
            at = i * SLOTS * PART
            pick_ref[at : at + SLOTS * PART, :] = jnp.concatenate(both, axis=0).astype(jnp.bfloat16)
        arrivals[s].wait()
        for h in range(PARTS):
            rows = x_ref[s, :, h].reshape(width, x_ref.shape[-1])
            got = jnp.dot(pick_ref[...], rows, preferred_element_type=jnp.float32)
            got = got.astype(jnp.bfloat16)
            for i in range(OG):
                at = i * SLOTS * PART
                to = h * SLOTS * PART
                o_ref[s * 8 + slots[i], to : to + SLOTS * PART, :] = got[at : at + SLOTS * PART]
        for copy in leaving[2 * s : 2 * s + 2]:
            copy.start()
    for copy in leaving:
        copy.wait()


def pack(screen, group, half_blocks):
    rows, orbitals, width = half_blocks.shape
    tiled = half_blocks.reshape(TILES, PARTS, PART, orbitals, width)
    kept = rows // TILES * SLOTS
    steps = orbitals // OG
    return pl.pallas_call(
        pack_kernel,
        in_specs=[
            pl.BlockSpec(memory_space=pltpu.SMEM),
            pl.BlockSpec(memory_space=pltpu.SMEM),
            pl.BlockSpec(memory_space=pl.ANY),
        ],
        out_specs=pl.BlockSpec(memory_space=pl.ANY),
        out_shape=jax.ShapeDtypeStruct((orbitals, kept, width), jnp.bfloat16),
        scratch_shapes=[
            pltpu.VMEM((steps, TILES, PARTS, PART, OG, width), jnp.bfloat16),
            pltpu.VMEM((orbitals, kept, width), jnp.bfloat16),
            pltpu.VMEM((OG * SLOTS * PART, TILES * PART * OG), jnp.bfloat16),
            pltpu.SMEM((TILES + 1, orbitals), jnp.int32),
            pltpu.SemaphoreType.DMA((steps,)),
            pltpu.SemaphoreType.DMA((2 * steps,)),
        ],
    )(screen, group, tiled)


def gram_kernel(place_ref, x_hbm, *refs):
    outs, x_ref, sems = refs[:SHARES], refs[-2], refs[-1]
    parts = sems.shape[0]
    depth = x_hbm.shape[0] // parts
    share = x_hbm.shape[1] // SHARES
    spans = [slice(p * depth, (p + 1) * depth) for p in range(parts)]
    arrivals = [
        pltpu.make_async_copy(x_hbm.at[span], x_ref.at[span], sems.at[p])
        for p, span in enumerate(spans)
    ]
    for copy in arrivals:
        copy.start()
    for p, span in enumerate(spans):
        arrivals[p].wait()
        left = []
        for shift in SHIFTS:
            start = pl.multiple_of((place_ref[0] ^ shift) * share, share)
            left.append(x_ref[span, pl.ds(start, share)])
        part = lax.dot_general(
            jnp.concatenate(left, axis=1),
            x_ref[span, :],
            (((0,), (0,)), ((), ())),
            preferred_element_type=jnp.float32,
        )
        for j in range(SHARES):
            piece = part[j * share : (j + 1) * share]
            if p == 0:
                outs[j][...] = piece
            else:
                outs[j][...] += piece


def gram(place, columns, parts=4):
    rows, width = columns.shape
    share = width // SHARES
    return pl.pallas_call(
        gram_kernel,
        in_specs=[pl.BlockSpec(memory_space=pltpu.SMEM), pl.BlockSpec(memory_space=pl.ANY)],
        out_specs=[pl.BlockSpec(memory_space=pltpu.VMEM)] * SHARES,
        out_shape=[jax.ShapeDtypeStruct((share, width), jnp.float32)] * SHARES,
        scratch_shapes=[
            pltpu.VMEM((rows, width), jnp.bfloat16),
            pltpu.SemaphoreType.DMA((parts,)),
        ],
    )(place, columns)


def routes(shift):
    pairs = []
    for g in range(4):
        for zh in range(4):
            for zl in range(2):
                for c in range(2):
                    pair, x = holder(zh, zl, c, g)
                    source = ((g * 2 + pair) * 2 + c) * 4 + x
                    pairs.append((source, ((zh * 2 + zl) * 2 + c) * 4 + (x ^ shift)))
    return pairs


def per_device(half_blocks, screen, domain_length, domain_index, orbital_coeff):
    dom_width = half_blocks.shape[2]
    group = lax.axis_index("zh").reshape(1)
    packed = pack(screen, group, half_blocks)
    arrived = lax.all_to_all(packed, ("zl", "y", "x", "c"), split_axis=0, concat_axis=0, tiled=True)
    columns = arrived.reshape(-1, dom_width)
    shares = gram(lax.axis_index("x").reshape(1), columns)
    total = None
    for share, shift in zip(shares, SHIFTS):
        got = lax.ppermute(share, ("zh", "zl", "c", "x"), routes(shift))
        total = got if total is None else total + got
    row_share = dom_width // SHARES
    length = domain_length[0]
    row_place = lax.axis_index("x") * row_share + lax.iota(jnp.int32, row_share)
    col_place = lax.iota(jnp.int32, dom_width)
    inside = ((row_place < length)[:, None] & (col_place < length)[None, :]).astype(jnp.float32)
    exch_rows = total * inside
    local_coeff = jnp.take(orbital_coeff, domain_index[0], axis=0).astype(jnp.float32)
    occ_rows = jnp.einsum("ab,bj->ja", exch_rows, local_coeff, precision=lax.Precision.HIGHEST)
    return (exch_rows[None], occ_rows[None])


def solution(mesh):
    split = Mesh(mesh.devices.reshape(4, 4, 2, 2, 4), ("y", "zh", "zl", "c", "x"))
    aux = ("y", "zh", "zl", "c")
    every = aux + ("x",)
    return jax.shard_map(
        per_device,
        mesh=split,
        in_specs=(P(every, None, None), P(every, None), P(aux), P(aux, None), P()),
        out_specs=(P(aux, "x", None), P(aux, None, "x")),
        check_vma=False,
    )
```

```python
import jax
import jax.numpy as jnp
from jax import lax
from jax.experimental import pallas as pl
from jax.experimental.pallas import tpu as pltpu
from jax.sharding import Mesh
from jax.sharding import PartitionSpec as P

TILES = 8
SLOTS = 4
PART = 4
PARTS = 4
OG = 16
SHARES = 4
SHIFTS = (2, 1, 3, 0)
NONE = -1000


def holder(zh, zl, c, g):
    away = (zh - g) & 3
    turn = (away + 1) & 3 if zl else away ^ 1
    return (1 - (away >> 1) if zl else (away ^ (away >> 1)) & 1), (turn - 2 * c) & 3


def slot_codes(screen_ref, code_ref, orbital):
    for k in range(SLOTS):
        code_ref[k, orbital] = NONE
    seen = 0
    for t in range(TILES):
        code_ref[seen, orbital] = t * PART * OG + orbital % OG
        seen = seen + screen_ref[t, orbital]
    code_ref[seen, orbital] = NONE


def pack_kernel(
    screen_ref, group_ref, x_hbm, o_hbm, x_ref, o_ref, pick_ref, code_ref, in_sems, out_sems
):
    steps = x_hbm.shape[3] // OG
    arrivals = [
        pltpu.make_async_copy(
            x_hbm.at[:, :, :, s * OG : (s + 1) * OG, :], x_ref.at[s], in_sems.at[s]
        )
        for s in range(steps)
    ]
    runs = [[(zl * steps + s) * 8 for zl in range(2)] for s in range(steps)]
    leaving = [
        pltpu.make_async_copy(
            o_ref.at[run : run + 8], o_hbm.at[run : run + 8], out_sems.at[run // 8]
        )
        for s in range(steps)
        for run in runs[s]
    ]
    for copy in arrivals:
        copy.start()
    slots = []
    for i in range(OG):
        pair, x = holder(i // 4, i // 2 % 2, i % 2, group_ref[0])
        slots.append(pair * steps * 8 + x * 2 + i % 2)
    width = TILES * PART * OG
    row = lax.broadcasted_iota(jnp.int32, (2 * PART, width), 0)
    place = lax.broadcasted_iota(jnp.int32, (2 * PART, width), 1) - OG * (row % PART)
    for s in range(steps):
        for i in range(OG):
            slot_codes(screen_ref, code_ref, s * OG + i)
        for i in range(OG):
            both = []
            for k in range(0, SLOTS, 2):
                first, second = (code_ref[k + d, s * OG + i] for d in range(2))
                both.append(jnp.where(place == jnp.where(row < PART, first, second), 1.0, 0.0))
            at = i * SLOTS * PART
            pick_ref[at : at + SLOTS * PART, :] = jnp.concatenate(both, axis=0).astype(jnp.bfloat16)
        arrivals[s].wait()
        for h in range(PARTS):
            rows = x_ref[s, :, h].reshape(width, x_ref.shape[-1])
            got = jnp.dot(pick_ref[...], rows, preferred_element_type=jnp.float32)
            got = got.astype(jnp.bfloat16)
            for i in range(OG):
                at = i * SLOTS * PART
                to = h * SLOTS * PART
                o_ref[s * 8 + slots[i], to : to + SLOTS * PART, :] = got[at : at + SLOTS * PART]
        for copy in leaving[2 * s : 2 * s + 2]:
            copy.start()
    for copy in leaving:
        copy.wait()


def pack(screen, group, half_blocks):
    rows, orbitals, width = half_blocks.shape
    tiled = half_blocks.reshape(TILES, PARTS, PART, orbitals, width)
    kept = rows // TILES * SLOTS
    steps = orbitals // OG
    return pl.pallas_call(
        pack_kernel,
        in_specs=[
            pl.BlockSpec(memory_space=pltpu.SMEM),
            pl.BlockSpec(memory_space=pltpu.SMEM),
            pl.BlockSpec(memory_space=pl.ANY),
        ],
        out_specs=pl.BlockSpec(memory_space=pl.ANY),
        out_shape=jax.ShapeDtypeStruct((orbitals, kept, width), jnp.bfloat16),
        scratch_shapes=[
            pltpu.VMEM((steps, TILES, PARTS, PART, OG, width), jnp.bfloat16),
            pltpu.VMEM((orbitals, kept, width), jnp.bfloat16),
            pltpu.VMEM((OG * SLOTS * PART, TILES * PART * OG), jnp.bfloat16),
            pltpu.SMEM((TILES + 1, orbitals), jnp.int32),
            pltpu.SemaphoreType.DMA((steps,)),
            pltpu.SemaphoreType.DMA((2 * steps,)),
        ],
    )(screen, group, tiled)


def gram_kernel(place_ref, x_hbm, *refs):
    outs, x_ref, sems = refs[:SHARES], refs[-2], refs[-1]
    parts = sems.shape[0]
    depth = x_hbm.shape[0] // parts
    share = x_hbm.shape[1] // SHARES
    spans = [slice(p * depth, (p + 1) * depth) for p in range(parts)]
    arrivals = [
        pltpu.make_async_copy(x_hbm.at[span], x_ref.at[span], sems.at[p])
        for p, span in enumerate(spans)
    ]
    for copy in arrivals:
        copy.start()
    for p, span in enumerate(spans):
        arrivals[p].wait()
        left = []
        for shift in SHIFTS:
            start = pl.multiple_of((place_ref[0] ^ shift) * share, share)
            left.append(x_ref[span, pl.ds(start, share)])
        part = lax.dot_general(
            jnp.concatenate(left, axis=1),
            x_ref[span, :],
            (((0,), (0,)), ((), ())),
            preferred_element_type=jnp.float32,
        )
        for j in range(SHARES):
            piece = part[j * share : (j + 1) * share]
            if p == 0:
                outs[j][...] = piece
            else:
                outs[j][...] += piece


def gram(place, columns, parts=4):
    rows, width = columns.shape
    share = width // SHARES
    return pl.pallas_call(
        gram_kernel,
        in_specs=[pl.BlockSpec(memory_space=pltpu.SMEM), pl.BlockSpec(memory_space=pl.ANY)],
        out_specs=[pl.BlockSpec(memory_space=pltpu.VMEM)] * SHARES,
        out_shape=[jax.ShapeDtypeStruct((share, width), jnp.float32)] * SHARES,
        scratch_shapes=[
            pltpu.VMEM((rows, width), jnp.bfloat16),
            pltpu.SemaphoreType.DMA((parts,)),
        ],
        compiler_params=pltpu.CompilerParams(vmem_limit_bytes=12 << 20),
    )(place, columns)


def routes(shift):
    pairs = []
    for g in range(4):
        for zh in range(4):
            for zl in range(2):
                for c in range(2):
                    pair, x = holder(zh, zl, c, g)
                    source = ((g * 2 + pair) * 2 + c) * 4 + x
                    pairs.append((source, ((zh * 2 + zl) * 2 + c) * 4 + (x ^ shift)))
    return pairs


def per_device(half_blocks, screen, domain_length, domain_index, orbital_coeff):
    dom_width = half_blocks.shape[2]
    group = lax.axis_index("zh").reshape(1)
    packed = pack(screen, group, half_blocks)
    arrived = lax.all_to_all(packed, ("zl", "y", "x", "c"), split_axis=0, concat_axis=0, tiled=True)
    columns = arrived.reshape(-1, dom_width)
    shares = gram(lax.axis_index("x").reshape(1), columns)
    total = None
    for share, shift in zip(shares, SHIFTS):
        got = lax.ppermute(share, ("zh", "zl", "c", "x"), routes(shift))
        total = got if total is None else total + got
    row_share = dom_width // SHARES
    length = domain_length[0]
    row_place = lax.axis_index("x") * row_share + lax.iota(jnp.int32, row_share)
    col_place = lax.iota(jnp.int32, dom_width)
    inside = ((row_place < length)[:, None] & (col_place < length)[None, :]).astype(jnp.float32)
    exch_rows = total * inside
    local_coeff = jnp.take(orbital_coeff, domain_index[0], axis=0).astype(jnp.float32)
    occ_rows = jnp.einsum("ab,bj->ja", exch_rows, local_coeff, precision=lax.Precision.HIGHEST)
    return (exch_rows[None], occ_rows[None])


def solution(mesh):
    split = Mesh(mesh.devices.reshape(4, 4, 2, 2, 4), ("y", "zh", "zl", "c", "x"))
    aux = ("y", "zh", "zl", "c")
    every = aux + ("x",)
    return jax.shard_map(
        per_device,
        mesh=split,
        in_specs=(P(every, None, None), P(every, None), P(aux), P(aux, None), P()),
        out_specs=(P(aux, "x", None), P(aux, None, "x")),
        check_vma=False,
    )
```

```python
import jax
import jax.numpy as jnp
from jax import lax
from jax.experimental import pallas as pl
from jax.experimental.pallas import tpu as pltpu
from jax.sharding import Mesh
from jax.sharding import PartitionSpec as P

TILES = 8
SLOTS = 4
PART = 4
PARTS = 4
OG = 16
SHARES = 4
SHIFTS = (2, 1, 3, 0)
NONE = -1000


def holder(zh, zl, c, g):
    away = (zh - g) & 3
    turn = (away + 1) & 3 if zl else away ^ 1
    return (1 - (away >> 1) if zl else (away ^ (away >> 1)) & 1), (turn - 2 * c) & 3


def slot_codes(screen_ref, code_ref, orbital):
    for k in range(SLOTS):
        code_ref[k, orbital] = NONE
    seen = 0
    for t in range(TILES):
        code_ref[seen, orbital] = t * PART * OG + orbital % OG
        seen = seen + screen_ref[t, orbital]
    code_ref[seen, orbital] = NONE


def pack_kernel(
    screen_ref, group_ref, x_hbm, o_hbm, x_ref, o_ref, pick_ref, code_ref, in_sems, out_sems
):
    steps = x_hbm.shape[3] // OG
    arrivals = [
        pltpu.make_async_copy(
            x_hbm.at[:, :, :, s * OG : (s + 1) * OG, :], x_ref.at[s], in_sems.at[s]
        )
        for s in range(steps)
    ]
    runs = [[(zl * steps + s) * 8 for zl in range(2)] for s in range(steps)]
    leaving = [
        pltpu.make_async_copy(
            o_ref.at[run : run + 8], o_hbm.at[run : run + 8], out_sems.at[run // 8]
        )
        for s in range(steps)
        for run in runs[s]
    ]
    for copy in arrivals:
        copy.start()
    slots = []
    for i in range(OG):
        pair, x = holder(i // 4, i // 2 % 2, i % 2, group_ref[0])
        slots.append(pair * steps * 8 + x * 2 + i % 2)
    width = TILES * PART * OG
    row = lax.broadcasted_iota(jnp.int32, (2 * PART, width), 0)
    place = lax.broadcasted_iota(jnp.int32, (2 * PART, width), 1) - OG * (row % PART)
    for s in range(steps):
        for i in range(OG):
            slot_codes(screen_ref, code_ref, s * OG + i)
        for i in range(OG):
            both = []
            for k in range(0, SLOTS, 2):
                first, second = (code_ref[k + d, s * OG + i] for d in range(2))
                both.append(jnp.where(place == jnp.where(row < PART, first, second), 1.0, 0.0))
            at = i * SLOTS * PART
            pick_ref[at : at + SLOTS * PART, :] = jnp.concatenate(both, axis=0).astype(jnp.bfloat16)
        arrivals[s].wait()
        for h in range(PARTS):
            rows = x_ref[s, :, h].reshape(width, x_ref.shape[-1])
            got = jnp.dot(pick_ref[...], rows, preferred_element_type=jnp.float32)
            got = got.astype(jnp.bfloat16)
            for i in range(OG):
                at = i * SLOTS * PART
                to = h * SLOTS * PART
                o_ref[s * 8 + slots[i], to : to + SLOTS * PART, :] = got[at : at + SLOTS * PART]
        for copy in leaving[2 * s : 2 * s + 2]:
            copy.start()
    for copy in leaving:
        copy.wait()


def pack(screen, group, half_blocks):
    rows, orbitals, width = half_blocks.shape
    tiled = half_blocks.reshape(TILES, PARTS, PART, orbitals, width)
    kept = rows // TILES * SLOTS
    steps = orbitals // OG
    return pl.pallas_call(
        pack_kernel,
        in_specs=[
            pl.BlockSpec(memory_space=pltpu.SMEM),
            pl.BlockSpec(memory_space=pltpu.SMEM),
            pl.BlockSpec(memory_space=pl.ANY),
        ],
        out_specs=pl.BlockSpec(memory_space=pl.ANY),
        out_shape=jax.ShapeDtypeStruct((orbitals, kept, width), jnp.bfloat16),
        scratch_shapes=[
            pltpu.VMEM((steps, TILES, PARTS, PART, OG, width), jnp.bfloat16),
            pltpu.VMEM((orbitals, kept, width), jnp.bfloat16),
            pltpu.VMEM((OG * SLOTS * PART, TILES * PART * OG), jnp.bfloat16),
            pltpu.SMEM((TILES + 1, orbitals), jnp.int32),
            pltpu.SemaphoreType.DMA((steps,)),
            pltpu.SemaphoreType.DMA((2 * steps,)),
        ],
    )(screen, group, tiled)


def gram_kernel(place_ref, x_hbm, *refs):
    outs, x_ref, sems = refs[:SHARES], refs[-2], refs[-1]
    parts = sems.shape[0]
    depth = x_hbm.shape[0] // parts
    share = x_hbm.shape[1] // SHARES
    spans = [slice(p * depth, (p + 1) * depth) for p in range(parts)]
    arrivals = [
        pltpu.make_async_copy(x_hbm.at[span], x_ref.at[span], sems.at[p])
        for p, span in enumerate(spans)
    ]
    for copy in arrivals:
        copy.start()
    for p, span in enumerate(spans):
        arrivals[p].wait()
        left = []
        for shift in SHIFTS:
            start = pl.multiple_of((place_ref[0] ^ shift) * share, share)
            left.append(x_ref[span, pl.ds(start, share)])
        part = lax.dot_general(
            jnp.concatenate(left, axis=1),
            x_ref[span, :],
            (((0,), (0,)), ((), ())),
            preferred_element_type=jnp.float32,
        )
        for j in range(SHARES):
            piece = part[j * share : (j + 1) * share]
            if p == 0:
                outs[j][...] = piece
            else:
                outs[j][...] += piece


def gram(place, columns, parts=4):
    rows, width = columns.shape
    share = width // SHARES
    return pl.pallas_call(
        gram_kernel,
        in_specs=[pl.BlockSpec(memory_space=pltpu.SMEM), pl.BlockSpec(memory_space=pl.ANY)],
        out_specs=[pl.BlockSpec(memory_space=pltpu.VMEM)] * SHARES,
        out_shape=[jax.ShapeDtypeStruct((share, width), jnp.float32)] * SHARES,
        scratch_shapes=[
            pltpu.VMEM((rows, width), jnp.bfloat16),
            pltpu.SemaphoreType.DMA((parts,)),
        ],
        compiler_params=pltpu.CompilerParams(vmem_limit_bytes=12 << 20),
    )(place, columns)


def routes(shift):
    pairs = []
    for g in range(4):
        for zh in range(4):
            for zl in range(2):
                for c in range(2):
                    pair, x = holder(zh, zl, c, g)
                    source = ((g * 2 + pair) * 2 + c) * 4 + x
                    pairs.append((source, ((zh * 2 + zl) * 2 + c) * 4 + (x ^ shift)))
    return pairs


def per_device(half_blocks, screen, domain_length, domain_index, orbital_coeff):
    dom_width = half_blocks.shape[2]
    group = lax.axis_index("zh").reshape(1)
    packed = pack(screen, group, half_blocks)
    arrived = lax.all_to_all(packed, ("zl", "y", "x", "c"), split_axis=0, concat_axis=0, tiled=True)
    local_coeff = jnp.take(orbital_coeff, domain_index[0], axis=0)
    arrived, local_coeff = lax.optimization_barrier((arrived, local_coeff))
    columns = arrived.reshape(-1, dom_width)
    shares = gram(lax.axis_index("x").reshape(1), columns)
    total = None
    for share, shift in zip(shares, SHIFTS):
        got = lax.ppermute(share, ("zh", "zl", "c", "x"), routes(shift))
        total = got if total is None else total + got
    row_share = dom_width // SHARES
    length = domain_length[0]
    row_place = lax.axis_index("x") * row_share + lax.iota(jnp.int32, row_share)
    col_place = lax.iota(jnp.int32, dom_width)
    inside = ((row_place < length)[:, None] & (col_place < length)[None, :]).astype(jnp.float32)
    exch_rows = total * inside
    local_coeff = local_coeff.astype(jnp.float32)
    occ_rows = jnp.einsum("ab,bj->ja", exch_rows, local_coeff, precision=lax.Precision.HIGHEST)
    return (exch_rows[None], occ_rows[None])


def solution(mesh):
    split = Mesh(mesh.devices.reshape(4, 4, 2, 2, 4), ("y", "zh", "zl", "c", "x"))
    aux = ("y", "zh", "zl", "c")
    every = aux + ("x",)
    return jax.shard_map(
        per_device,
        mesh=split,
        in_specs=(P(every, None, None), P(every, None), P(aux), P(aux, None), P()),
        out_specs=(P(aux, "x", None), P(aux, None, "x")),
        check_vma=False,
    )
```

```python
import functools

import jax
import jax.numpy as jnp
from jax import lax
from jax.experimental import pallas as pl
from jax.experimental.pallas import tpu as pltpu
from jax.sharding import Mesh
from jax.sharding import PartitionSpec as P

TILES = 8
SLOTS = 4
PART = 4
PARTS = 4
OG = 16
SHARES = 4
SHIFTS = (1, 2, 3, 0)
NONE = -1000


def holder(zh, zl, c, g):
    away = (zh - g) & 3
    turn = (away + 1) & 3 if zl else away ^ 1
    return (1 - (away >> 1) if zl else (away ^ (away >> 1)) & 1), (turn - 2 * c) & 3


def slot_codes(screen_ref, code_ref, orbital):
    for k in range(SLOTS):
        code_ref[k, orbital] = NONE
    seen = 0
    for t in range(TILES):
        code_ref[seen, orbital] = t * PART * OG + orbital % OG
        seen = seen + screen_ref[t, orbital]
    code_ref[seen, orbital] = NONE


def pack_kernel(
    screen_ref, group_ref, x_hbm, o_hbm, x_ref, o_ref, pick_ref, code_ref, in_sems, out_sems
):
    steps = x_hbm.shape[3] // OG
    arrivals = [
        pltpu.make_async_copy(
            x_hbm.at[:, :, :, s * OG : (s + 1) * OG, :], x_ref.at[s], in_sems.at[s]
        )
        for s in range(steps)
    ]
    runs = [[(zl * steps + s) * 8 for zl in range(2)] for s in range(steps)]
    leaving = [
        pltpu.make_async_copy(
            o_ref.at[run : run + 8], o_hbm.at[run : run + 8], out_sems.at[run // 8]
        )
        for s in range(steps)
        for run in runs[s]
    ]
    for copy in arrivals:
        copy.start()
    slots = []
    for i in range(OG):
        pair, x = holder(i // 4, i // 2 % 2, i % 2, group_ref[0])
        slots.append(pair * steps * 8 + x * 2 + i % 2)
    width = TILES * PART * OG
    row = lax.broadcasted_iota(jnp.int32, (2 * PART, width), 0)
    place = lax.broadcasted_iota(jnp.int32, (2 * PART, width), 1) - OG * (row % PART)
    for s in range(steps):
        for i in range(OG):
            slot_codes(screen_ref, code_ref, s * OG + i)
        for i in range(OG):
            both = []
            for k in range(0, SLOTS, 2):
                first, second = (code_ref[k + d, s * OG + i] for d in range(2))
                both.append(jnp.where(place == jnp.where(row < PART, first, second), 1.0, 0.0))
            at = i * SLOTS * PART
            pick_ref[at : at + SLOTS * PART, :] = jnp.concatenate(both, axis=0).astype(jnp.bfloat16)
        arrivals[s].wait()
        for h in range(PARTS):
            rows = x_ref[s, :, h].reshape(width, x_ref.shape[-1])
            got = jnp.dot(pick_ref[...], rows, preferred_element_type=jnp.float32)
            got = got.astype(jnp.bfloat16)
            for i in range(OG):
                at = i * SLOTS * PART
                to = h * SLOTS * PART
                o_ref[s * 8 + slots[i], to : to + SLOTS * PART, :] = got[at : at + SLOTS * PART]
        for copy in leaving[2 * s : 2 * s + 2]:
            copy.start()
    for copy in leaving:
        copy.wait()


def pack(screen, group, half_blocks):
    rows, orbitals, width = half_blocks.shape
    tiled = half_blocks.reshape(TILES, PARTS, PART, orbitals, width)
    kept = rows // TILES * SLOTS
    steps = orbitals // OG
    return pl.pallas_call(
        pack_kernel,
        in_specs=[
            pl.BlockSpec(memory_space=pltpu.SMEM),
            pl.BlockSpec(memory_space=pltpu.SMEM),
            pl.BlockSpec(memory_space=pl.ANY),
        ],
        out_specs=pl.BlockSpec(memory_space=pl.ANY),
        out_shape=jax.ShapeDtypeStruct((orbitals, kept, width), jnp.bfloat16),
        scratch_shapes=[
            pltpu.VMEM((steps, TILES, PARTS, PART, OG, width), jnp.bfloat16),
            pltpu.VMEM((orbitals, kept, width), jnp.bfloat16),
            pltpu.VMEM((OG * SLOTS * PART, TILES * PART * OG), jnp.bfloat16),
            pltpu.SMEM((TILES + 1, orbitals), jnp.int32),
            pltpu.SemaphoreType.DMA((steps,)),
            pltpu.SemaphoreType.DMA((2 * steps,)),
        ],
    )(screen, group, tiled)


def gram_kernel(shifts, place_ref, x_hbm, *refs):
    outs, x_ref, sems = refs[: len(shifts)], refs[-2], refs[-1]
    parts = sems.shape[0]
    depth = x_hbm.shape[0] // parts
    share = x_hbm.shape[1] // SHARES
    spans = [slice(p * depth, (p + 1) * depth) for p in range(parts)]
    arrivals = [
        pltpu.make_async_copy(x_hbm.at[span], x_ref.at[span], sems.at[p])
        for p, span in enumerate(spans)
    ]
    for copy in arrivals:
        copy.start()
    for p, span in enumerate(spans):
        arrivals[p].wait()
        left = []
        for shift in shifts:
            start = pl.multiple_of((place_ref[0] ^ shift) * share, share)
            left.append(x_ref[span, pl.ds(start, share)])
        part = lax.dot_general(
            jnp.concatenate(left, axis=1),
            x_ref[span, :],
            (((0,), (0,)), ((), ())),
            preferred_element_type=jnp.float32,
        )
        for j in range(len(shifts)):
            piece = part[j * share : (j + 1) * share]
            if p == 0:
                outs[j][...] = piece
            else:
                outs[j][...] += piece


def gram(place, columns, shifts, parts=4):
    rows, width = columns.shape
    share = width // SHARES
    return pl.pallas_call(
        functools.partial(gram_kernel, shifts),
        in_specs=[pl.BlockSpec(memory_space=pltpu.SMEM), pl.BlockSpec(memory_space=pl.ANY)],
        out_specs=[pl.BlockSpec(memory_space=pltpu.VMEM)] * len(shifts),
        out_shape=[jax.ShapeDtypeStruct((share, width), jnp.float32)] * len(shifts),
        scratch_shapes=[
            pltpu.VMEM((rows, width), jnp.bfloat16),
            pltpu.SemaphoreType.DMA((parts,)),
        ],
        compiler_params=pltpu.CompilerParams(vmem_limit_bytes=12 << 20),
        cost_estimate=pl.CostEstimate(
            flops=2 * rows * width * share * len(shifts),
            bytes_accessed=2 * rows * width,
            transcendentals=0,
        ),
    )(place, columns)


def routes(shift):
    pairs = []
    for g in range(4):
        for zh in range(4):
            for zl in range(2):
                for c in range(2):
                    pair, x = holder(zh, zl, c, g)
                    source = ((g * 2 + pair) * 2 + c) * 4 + x
                    pairs.append((source, ((zh * 2 + zl) * 2 + c) * 4 + (x ^ shift)))
    return pairs


def per_device(half_blocks, screen, domain_length, domain_index, orbital_coeff):
    dom_width = half_blocks.shape[2]
    group = lax.axis_index("zh").reshape(1)
    packed = pack(screen, group, half_blocks)
    arrived = lax.all_to_all(packed, ("zl", "y", "x", "c"), split_axis=0, concat_axis=0, tiled=True)
    local_coeff = jnp.take(orbital_coeff, domain_index[0], axis=0)
    arrived, local_coeff = lax.optimization_barrier((arrived, local_coeff))
    columns = arrived.reshape(-1, dom_width)
    place = lax.axis_index("x").reshape(1)
    total = None
    for part in range(2):
        shifts = SHIFTS[2 * part : 2 * part + 2]
        shares = gram(place, columns, shifts)
        for share, shift in zip(shares, shifts):
            got = lax.ppermute(share, ("zh", "zl", "c", "x"), routes(shift))
            total = got if total is None else total + got
    row_share = dom_width // SHARES
    length = domain_length[0]
    row_place = lax.axis_index("x") * row_share + lax.iota(jnp.int32, row_share)
    col_place = lax.iota(jnp.int32, dom_width)
    inside = ((row_place < length)[:, None] & (col_place < length)[None, :]).astype(jnp.float32)
    exch_rows = total * inside
    local_coeff = local_coeff.astype(jnp.float32)
    occ_rows = jnp.einsum("ab,bj->ja", exch_rows, local_coeff, precision=lax.Precision.HIGHEST)
    return (exch_rows[None], occ_rows[None])


def solution(mesh):
    split = Mesh(mesh.devices.reshape(4, 4, 2, 2, 4), ("y", "zh", "zl", "c", "x"))
    aux = ("y", "zh", "zl", "c")
    every = aux + ("x",)
    return jax.shard_map(
        per_device,
        mesh=split,
        in_specs=(P(every, None, None), P(every, None), P(aux), P(aux, None), P()),
        out_specs=(P(aux, "x", None), P(aux, None, "x")),
        check_vma=False,
    )
```
